32 devices in a mesh: cell: 8 (over y, x, core), chan: 4 (over z).
Axes of the slice: x: 2, y: 2, z: 4, core: 2. Of those that a mesh axis runs over, the one named last changes fastest.
Arguments:
- embeds: float32 [32768, 512], P('cell', 'chan'), may hold values from -260 to 260
Outputs:
- whitened: float32 [32768, 512], P(('cell', 'chan'))
- factor: float32 [512, 512], replicated
The draws below stay inside these ranges and needn't reach their ends.
All inputs are finite; a program needn't handle non-finite values.
Results may differ from the reference program's by a relative error of at most 0.000088.
Values sent between devices are 32-bit elements; how exact they have to be, the bound alone decides.
No kernel may reach another device: no remote copies, remote signals or barrier semaphores. Data moves between devices by JAX's collectives and lax.ppermute only.
A program may use at most 64 MiB of HBM per device.

```python
import math
import jax
import jax.numpy as jnp
from jax import lax

D = 512
ROWS = 32768


def draw_embeds(key, part):
    key_base = jax.random.fold_in(key, 11)
    key_rows = jax.random.fold_in(key, 12)
    key_cols = jax.random.fold_in(key, 13)
    base = jnp.clip(jax.random.normal(key_base, (ROWS, D), jnp.float32), -6.0, 6.0)
    row_scale = jnp.exp(jax.random.uniform(key_rows, (ROWS, 1), jnp.float32) * math.log(10.0))
    ramp = jnp.sqrt(1.0 + 2.0 * jnp.arange(ROWS, dtype=jnp.float32)[:, None] / ROWS)
    col_scale = jnp.exp(jax.random.uniform(key_cols, (1, D), jnp.float32) * math.log(10.0))
    return 0.25 * base * row_scale * ramp * col_scale


def setup_inputs(seed: int = 0) -> dict:
    key_list = jax.random.split(jax.random.key(seed), 2)
    embeds = draw_embeds(jax.random.fold_in(key_list[1], 71), 0)
    return dict(embeds=embeds)


def reference(embeds):
    gram = lax.dot_general(embeds.astype(jnp.float32), embeds.astype(jnp.float32), (((0,), (0,)), ((), ())), precision=lax.Precision.HIGHEST, preferred_element_type=jnp.float32)
    lower = jnp.linalg.cholesky(gram)
    scale = jnp.sqrt(jnp.asarray(ROWS, dtype=gram.dtype))
    whitened = jax.scipy.linalg.solve_triangular(lower, embeds.T, lower=True).T * scale
    return (whitened, lower.T / scale)
```

```python
import math

import jax
import jax.numpy as jnp
from jax import lax
from jax.experimental import pallas as pl
from jax.experimental.pallas import tpu as pltpu
from jax.sharding import PartitionSpec as P


LANES = 128
CHUNKS = 4
STEPS = 8
TOL = 2e-6
F32 = jnp.float32
BF16 = jnp.bfloat16


def split2(x):
    high = x.astype(BF16)
    return high, (x - high.astype(F32)).astype(BF16)


def split3(x):
    high = x.astype(BF16)
    rest = x - high.astype(F32)
    mid = rest.astype(BF16)
    return high, mid, (rest - mid.astype(F32)).astype(BF16)


def dot(a, b, dims):
    return lax.dot_general(a, b, (dims, ((), ())), preferred_element_type=F32)


NN = ((1,), (0,))
NT = ((1,), (1,))
TN = ((0,), (0,))


def dot3(a, b, dims):
    return dot(a[0], b[1], dims) + dot(a[1], b[0], dims) + dot(a[0], b[0], dims)


def dot6(a, b, dims):
    small = dot(a[0], b[2], dims) + dot(a[2], b[0], dims) + dot(a[1], b[1], dims)
    return small + (dot(a[0], b[1], dims) + dot(a[1], b[0], dims)) + dot(a[0], b[0], dims)


def upper_blocks(n):
    return [(p, q) for p in range(n) for q in range(p, n)]


def gram_kernel(count, first, z_ref, *refs):
    pieces = refs[:count]
    before = None if first else refs[count]
    gram, high, mid, low = refs[count + (0 if first else 1) :]
    width = pieces[0].shape[1]
    for a in range(count):
        lanes = slice(None)
        if count > 1:
            lanes = pl.ds(pl.multiple_of((z_ref[0] ^ a) * width, width), width)
        high[:, lanes], mid[:, lanes], low[:, lanes] = split3(pieces[a][...])
    n = high.shape[1] // LANES
    place = {pq: i for i, pq in enumerate(upper_blocks(n))}
    for p in range(n):
        rows = slice(p * LANES, (p + 1) * LANES)
        rest = slice(p * LANES, n * LANES)
        lhs = (high[:, rows], mid[:, rows], low[:, rows])
        rhs = (high[:, rest], mid[:, rest], low[:, rest])
        value = dot6(lhs, rhs, TN)
        for q in range(p, n):
            at = slice(place[p, q] * LANES, (place[p, q] + 1) * LANES)
            block = value[:, (q - p) * LANES : (q - p + 1) * LANES]
            gram[at, :] = block if first else before[at, :] + block


def partial_gram(z, pieces, before):
    rows = pieces[0].shape[0]
    depth = sum(p.shape[1] for p in pieces)
    n = depth // LANES
    size = len(upper_blocks(n)) * LANES
    part = jax.ShapeDtypeStruct((rows, depth), BF16)
    vmem = pl.BlockSpec(memory_space=pltpu.VMEM)
    args = list(pieces) + ([] if before is None else [before])

    def kernel(*refs):
        gram_kernel(len(pieces), before is None, *refs)

    return pl.pallas_call(
        kernel,
        out_shape=(jax.ShapeDtypeStruct((size, LANES), F32), part, part, part),
        in_specs=[pl.BlockSpec(memory_space=pltpu.SMEM)] + [vmem] * len(args),
        out_specs=(vmem,) * 4,
        input_output_aliases={} if before is None else {len(args): 0},
        cost_estimate=pl.CostEstimate(
            flops=12 * rows * depth * depth, bytes_accessed=16 * rows * depth, transcendentals=0
        ),
    )(z, *args)


def factor_kernel(chunks, scale, blocks, *refs):
    parts = refs[: 3 * chunks]
    whitened, factor, gram, gram_high, gram_low, inverse, product, phi, good = refs[3 * chunks :]
    depth = gram.shape[0]
    n = depth // LANES
    half = depth // 2
    top, bottom = slice(0, half), slice(half, depth)
    row = lax.broadcasted_iota(jnp.int32, (depth, depth), 0)
    lane = lax.broadcasted_iota(jnp.int32, (depth, depth), 1)

    for i, (p, q) in enumerate(upper_blocks(n)):
        block = blocks[i * LANES : (i + 1) * LANES, :]
        gram[p * LANES : (p + 1) * LANES, q * LANES : (q + 1) * LANES] = block
        if p < q:
            gram[q * LANES : (q + 1) * LANES, p * LANES : (p + 1) * LANES] = block.T
    diagonal = jnp.where(row == lane, gram[...], 0.0)
    across = lax.rsqrt(jnp.sum(diagonal, axis=0, keepdims=True))
    down = lax.rsqrt(jnp.sum(diagonal, axis=1, keepdims=True))
    scaled = gram[...] * across * down
    gram[...] = scaled
    gram_high[...], gram_low[...] = split2(scaled)
    inverse[...] = jnp.where(row == lane, 1.0, jnp.where(row > lane, -scaled, 0.0))

    def correction(block, diagonal):
        if not diagonal:
            return block, block
        r = lax.broadcasted_iota(jnp.int32, block.shape, 0)
        c = lax.broadcasted_iota(jnp.int32, block.shape, 1)
        error = jnp.where(r == c, block - 1.0, block)
        kept = jnp.where(r > c, error, jnp.where(r == c, 0.5 * error, 0.0))
        return kept, kept

    def step(three):
        def mm(a, b, dims):
            return dot3(a, b, dims) if three else dot(a[0], b[0], dims)

        def pair(ref, r, c):
            return (ref[0][r, c], ref[1][r, c])

        x = split2(inverse[...])
        g = (gram_high, gram_low)
        x00 = (x[0][top, top], x[1][top, top])
        x1 = (x[0][bottom, :], x[1][bottom, :])
        a0 = mm(x00, pair(g, top, slice(None)), NN)
        a1 = mm(x1, pair(g, slice(None), slice(None)), NN)
        product[top, :] = a0
        product[bottom, :] = a1
        a00 = split2(a0[:, top])
        a1s = split2(a1)
        m00 = mm(a00, x00, NT)
        m10 = mm((a1s[0][:, top], a1s[1][:, top]), x00, NT)
        m11 = mm(a1s, x1, NT)
        p00, _ = correction(m00, True)
        p10, _ = correction(m10, False)
        p11, _ = correction(m11, True)
        error = jnp.sum(p00 * p00) + jnp.sum(p10 * p10) + jnp.sum(p11 * p11)
        p00, p10, p11 = p00.astype(BF16), p10.astype(BF16), p11.astype(BF16)
        phi[top, top] = p00
        phi[bottom, top] = p10
        phi[bottom, bottom] = p11
        inverse[top, top] = inverse[top, top] - dot(p00, x[0][top, top], NN)
        inverse[bottom, top] = (
            inverse[bottom, top] - dot(p10, x[0][top, top], NN) - dot(p11, x[0][bottom, top], NN)
        )
        inverse[bottom, bottom] = inverse[bottom, bottom] - dot(p11, x[0][bottom, bottom], NN)
        return error

    step(False)
    _, error = lax.while_loop(
        lambda c: (c[0] < STEPS) & (c[1] > TOL),
        lambda c: (c[0] + 1, step(True)),
        (jnp.int32(0), F32(1.0)),
    )
    converged = error <= TOL

    @pl.when(converged)
    def _():
        a = product[...]
        ah = a.astype(BF16)
        product[top, :] = a[top, :] - dot(phi[top, top], ah[top, :], NN)
        product[bottom, :] = a[bottom, :] - dot(phi[bottom, :], ah, NN)

    @pl.when(jnp.logical_not(converged))
    def _():
        product[...] = gram[...]
        inverse[...] = jnp.where(row == lane, 1.0, 0.0)
        lane_row = lax.broadcasted_iota(jnp.int32, (1, depth), 1)
        row_column = lax.broadcasted_iota(jnp.int32, (depth, 1), 0)

        def eliminate(k, carry):
            pivot_row = product[pl.ds(k, 1), :]
            inverse_row = inverse[pl.ds(k, 1), :]
            pivot = jnp.sum(jnp.where(lane_row == k, pivot_row, 0.0), axis=1, keepdims=True)
            column = jnp.sum(jnp.where(lane == k, product[...], 0.0), axis=1, keepdims=True)
            ratio = jnp.where(row_column > k, column / pivot, 0.0)
            product[...] = product[...] - ratio * pivot_row
            inverse[...] = inverse[...] - ratio * inverse_row
            return carry

        lax.fori_loop(0, depth, eliminate, 0)
        pivots = jnp.sum(jnp.where(row == lane, product[...], 0.0), axis=1, keepdims=True)
        root = 1.0 / jnp.sqrt(pivots)
        product[...] = product[...] * root
        inverse[...] = inverse[...] * root

    factor[...] = jnp.where(row <= lane, product[...], 0.0) * (1.0 / (across * scale))
    x = split3(jnp.where(row >= lane, inverse[...], 0.0) * (across * scale))
    x00 = tuple(v[top, top] for v in x)
    x1 = tuple(v[bottom, :] for v in x)
    at = 0
    for c in range(chunks):
        part = parts[3 * c : 3 * c + 3]
        size = part[0].shape[0]
        out = slice(at, at + size)
        whitened[out, top] = dot6([v[:, top] for v in part], x00, NT)
        whitened[out, bottom] = dot6([v[...] for v in part], x1, NT)
        at += size


def factor_and_apply(blocks, parts, scale):
    depth = parts[0].shape[1]
    chunks = len(parts) // 3
    rows = sum(p.shape[0] for p in parts[::3])
    square = jax.ShapeDtypeStruct((depth, depth), F32)
    vmem = pl.BlockSpec(memory_space=pltpu.VMEM)

    def kernel(*refs):
        factor_kernel(chunks, scale, *refs)

    return pl.pallas_call(
        kernel,
        out_shape=(jax.ShapeDtypeStruct((rows, depth), F32), square),
        in_specs=[vmem] * (1 + len(parts)),
        out_specs=(vmem, vmem),
        scratch_shapes=[
            pltpu.VMEM((depth, depth), F32),
            pltpu.VMEM((depth, depth), BF16),
            pltpu.VMEM((depth, depth), BF16),
            pltpu.VMEM((depth, depth), F32),
            pltpu.VMEM((depth, depth), F32),
            pltpu.VMEM((depth, depth), BF16),
            pltpu.SMEM((1,), jnp.int32),
        ],
        cost_estimate=pl.CostEstimate(
            flops=40 * depth**3, bytes_accessed=16 * rows * depth, transcendentals=0
        ),
    )(blocks, *parts)


def take(x, i):
    return lax.dynamic_index_in_dim(x, i, 0, keepdims=False)


def swap(x, axis, distance):
    return lax.ppermute(x, axis, [(i, i ^ distance) for i in range(lax.axis_size(axis))])


def scatter_sum(x, axis, index, count, stride):
    shares = x.reshape(count, x.shape[0] // count, x.shape[1])
    total = take(shares, index)
    arrived = [swap(take(shares, index ^ k), axis, k * stride) for k in range(1, count)]
    for value in arrived:
        total = total + value
    return total


def gather(x, axis, index, count, stride):
    arrived = [x] + [swap(x, axis, k * stride) for k in range(1, count)]
    out = jnp.zeros((count,) + x.shape, x.dtype)
    for k in range(count):
        out = lax.dynamic_update_index_in_dim(out, arrived[k], index ^ k, 0)
    return out.reshape(count * x.shape[0], x.shape[1])


def reduce_blocks(x):
    cell, z = lax.axis_index("cell"), lax.axis_index("chan")
    cells, count = lax.axis_size("cell"), lax.axis_size("chan")
    core, chip, chips = cell % 2, cell // 2, cells // 2
    x = scatter_sum(x, "cell", core, 2, 1)
    x = scatter_sum(x, "cell", chip, chips, 2)
    arrived = [x] + [swap(x, "chan", k) for k in range(1, count)]
    while len(arrived) > 1:
        arrived = [arrived[i] + arrived[i + 1] for i in range(0, len(arrived), 2)]
    x = gather(arrived[0], "cell", chip, chips, 2)
    return gather(x, "cell", core, 2, 1)


def per_device(embeds):
    z = lax.axis_index("chan")
    count = lax.axis_size("chan")
    rows, width = embeds.shape[0] // count, embeds.shape[1]
    chunks = CHUNKS
    size = rows // chunks
    if width % LANES == 0:
        owned = embeds.reshape(count, chunks, size, width)
        pieces = [
            [
                v if k == 0 else swap(v, "chan", k)
                for k in range(count)
                for v in [take(owned[:, c], z ^ k)]
            ]
            for c in range(chunks)
        ]
    else:
        whole = lax.all_to_all(embeds, "chan", split_axis=0, concat_axis=1, tiled=True)
        pieces = [[whole[c * size : (c + 1) * size]] for c in range(chunks)]
    index = jnp.reshape(z, (1,)).astype(jnp.int32)
    gram, parts = None, []
    for c in range(chunks):
        gram, *split = partial_gram(index, pieces[c], gram)
        parts += split
    gram = reduce_blocks(gram)
    total = rows * lax.axis_size("cell") * count
    return factor_and_apply(gram, parts, math.sqrt(total))


def solution(mesh):
    in_specs = (P("cell", "chan"),)
    out_specs = (P(("cell", "chan"), None), P())
    return jax.shard_map(
        per_device, mesh=mesh, in_specs=in_specs, out_specs=out_specs, check_vma=False
    )
```

```python
import math

import jax
import jax.numpy as jnp
from jax import lax
from jax.experimental import pallas as pl
from jax.experimental.pallas import tpu as pltpu
from jax.sharding import PartitionSpec as P


LANES = 128
CHUNKS = 4
STEPS = 8
TOL = 2e-6
GRAM_VMEM = 12 << 20
FACTOR_VMEM = 24 << 20
SMALL_VMEM = 4 << 20
F32 = jnp.float32
BF16 = jnp.bfloat16


def split2(x):
    high = x.astype(BF16)
    return high, (x - high.astype(F32)).astype(BF16)


def split3(x):
    high = x.astype(BF16)
    rest = x - high.astype(F32)
    mid = rest.astype(BF16)
    return high, mid, (rest - mid.astype(F32)).astype(BF16)


def dot(a, b, dims):
    return lax.dot_general(a, b, (dims, ((), ())), preferred_element_type=F32)


NN = ((1,), (0,))
NT = ((1,), (1,))
TN = ((0,), (0,))


def dot3(a, b, dims):
    return dot(a[0], b[1], dims) + dot(a[1], b[0], dims) + dot(a[0], b[0], dims)


def dot6(a, b, dims):
    small = dot(a[0], b[2], dims) + dot(a[2], b[0], dims) + dot(a[1], b[1], dims)
    return small + (dot(a[0], b[1], dims) + dot(a[1], b[0], dims)) + dot(a[0], b[0], dims)


def upper_blocks(n):
    return [(p, q) for p in range(n) for q in range(p, n)]


def position():
    cell = lax.axis_index("cell")
    return lax.axis_index("chan"), cell & 1, lax.shift_right_logical(cell, 1)


def gram_kernel(count, first, last, *refs):
    z, core, _ = position()
    pieces = refs[:count]
    before = None if first else refs[count]
    refs = refs[count + (0 if first else 1) :]
    if last:
        kept, sent, gram, high, mid, low = refs
    else:
        gram, high, mid, low = refs
    width = pieces[0].shape[1]
    for a in range(count):
        lanes = slice(None)
        if count > 1:
            lanes = pl.ds(pl.multiple_of((z ^ a) * width, width), width)
        high[:, lanes], mid[:, lanes], low[:, lanes] = split3(pieces[a][...])
    n = high.shape[1] // LANES
    place = {pq: i for i, pq in enumerate(upper_blocks(n))}
    wide = 2
    for top in range(0, n, wide):
        rows = slice(top * LANES, (top + wide) * LANES)
        rest = slice(top * LANES, n * LANES)
        lhs = (high[:, rows], mid[:, rows], low[:, rows])
        rhs = (high[:, rest], mid[:, rest], low[:, rest])
        value = dot6(lhs, rhs, TN)
        for p in range(top, top + wide):
            for q in range(p, n):
                at = slice(place[p, q] * LANES, (place[p, q] + 1) * LANES)
                down = slice((p - top) * LANES, (p - top + 1) * LANES)
                block = value[down, (q - top) * LANES : (q - top + 1) * LANES]
                gram[at, :] = block if first else before[at, :] + block
    if last:
        size = kept.shape[0]
        kept[...] = gram[pl.ds(pl.multiple_of(core * size, 8), size), :]
        sent[...] = gram[pl.ds(pl.multiple_of((1 - core) * size, 8), size), :]


VMEM = pl.BlockSpec(memory_space=pltpu.VMEM)
HBM = pl.BlockSpec(memory_space=pltpu.HBM)


def partial_gram(pieces, before, last):
    rows = pieces[0].shape[0]
    depth = sum(p.shape[1] for p in pieces)
    size = len(upper_blocks(depth // LANES)) * LANES
    args = list(pieces) + ([] if before is None else [before])

    def kernel(*refs):
        gram_kernel(len(pieces), before is None, last, *refs)

    whole = jax.ShapeDtypeStruct((size, LANES), F32)
    part = jax.ShapeDtypeStruct((size // 2, LANES), F32)
    return pl.pallas_call(
        kernel,
        out_shape=(part, part) if last else whole,
        in_specs=[VMEM] * len(args),
        out_specs=(VMEM, VMEM) if last else VMEM,
        scratch_shapes=([pltpu.VMEM((size, LANES), F32)] if last else [])
        + [pltpu.VMEM((rows, depth), BF16)] * 3,
        input_output_aliases={} if before is None or last else {len(args) - 1: 0},
        compiler_params=pltpu.CompilerParams(vmem_limit_bytes=GRAM_VMEM),
        cost_estimate=pl.CostEstimate(
            flops=12 * rows * depth * depth, bytes_accessed=16 * rows * depth, transcendentals=0
        ),
    )(*args)


def factor_kernel(sizes, count, scale, mine, other, *refs):
    z, core, _ = position()
    pieces = refs[: len(sizes) * count]
    refs = refs[len(pieces) :]
    whitened, factor, blocks, gram, gram_high, gram_low, inverse, product, phi, rows_in, rows_out, sem_in, sem_out = refs
    depth = gram.shape[0]
    n = depth // LANES
    half = depth // 2
    top, bottom = slice(0, half), slice(half, depth)
    row = lax.broadcasted_iota(jnp.int32, (depth, depth), 0)
    lane = lax.broadcasted_iota(jnp.int32, (depth, depth), 1)

    starts = [sum(sizes[:c]) for c in range(len(sizes))]
    copies = []
    for i, piece in enumerate(pieces):
        c, k = i // count, i % count
        width = piece.shape[1]
        lanes = slice(None)
        if count > 1:
            lanes = pl.ds(pl.multiple_of((z ^ k) * width, width), width)
        target = rows_in.at[pl.ds(starts[c], sizes[c]), lanes]
        copies.append(pltpu.make_async_copy(piece, target, sem_in.at[i]))
    for copy in copies:
        copy.start()

    size = mine.shape[0]
    blocks[pl.ds(pl.multiple_of(core * size, 8), size), :] = mine[...]
    blocks[pl.ds(pl.multiple_of((1 - core) * size, 8), size), :] = other[...]
    for i, (p, q) in enumerate(upper_blocks(n)):
        block = blocks[i * LANES : (i + 1) * LANES, :]
        gram[p * LANES : (p + 1) * LANES, q * LANES : (q + 1) * LANES] = block
        if p < q:
            gram[q * LANES : (q + 1) * LANES, p * LANES : (p + 1) * LANES] = block.T
    diagonal = jnp.where(row == lane, gram[...], 0.0)
    across = lax.rsqrt(jnp.sum(diagonal, axis=0, keepdims=True))
    down = lax.rsqrt(jnp.sum(diagonal, axis=1, keepdims=True))
    scaled = gram[...] * across * down
    gram[...] = scaled
    gram_high[...], gram_low[...] = split2(scaled)
    inverse[...] = jnp.where(row == lane, 1.0, jnp.where(row > lane, -scaled, 0.0))

    def correction(block):
        r = lax.broadcasted_iota(jnp.int32, block.shape, 0)
        c = lax.broadcasted_iota(jnp.int32, block.shape, 1)
        return jnp.where(r > c, block, jnp.where(r == c, 0.5 * (block - 1.0), 0.0))

    def step(three):
        def mm(a, b, dims):
            return dot3(a, b, dims) if three else dot(a[0], b[0], dims)

        x = split2(inverse[...])
        x00 = (x[0][top, top], x[1][top, top])
        x1 = (x[0][bottom, :], x[1][bottom, :])
        a0 = mm(x00, (gram_high[top, :], gram_low[top, :]), NN)
        a1 = mm(x1, (gram_high[...], gram_low[...]), NN)
        product[top, :] = a0
        product[bottom, :] = a1
        a00 = split2(a0[:, top])
        a1s = split2(a1)
        p00 = correction(mm(a00, x00, NT))
        p10 = mm((a1s[0][:, top], a1s[1][:, top]), x00, NT)
        p11 = correction(mm(a1s, x1, NT))
        error = jnp.sum(p00 * p00) + jnp.sum(p10 * p10) + jnp.sum(p11 * p11)
        p00, p10, p11 = p00.astype(BF16), p10.astype(BF16), p11.astype(BF16)
        phi[top, top] = p00
        phi[bottom, top] = p10
        phi[bottom, bottom] = p11
        inverse[top, top] = inverse[top, top] - dot(p00, x[0][top, top], NN)
        inverse[bottom, top] = (
            inverse[bottom, top] - dot(p10, x[0][top, top], NN) - dot(p11, x[0][bottom, top], NN)
        )
        inverse[bottom, bottom] = inverse[bottom, bottom] - dot(p11, x[0][bottom, bottom], NN)
        return error

    step(False)
    _, error = lax.while_loop(
        lambda c: (c[0] < STEPS) & (c[1] > TOL),
        lambda c: (c[0] + 1, step(True)),
        (jnp.int32(0), F32(1.0)),
    )
    converged = error <= TOL

    def finish(exact):
        factor[...] = jnp.where(row <= lane, product[...], 0.0) * (1.0 / (across * scale))
        x = jnp.where(row >= lane, inverse[...], 0.0) * (across * scale)
        split, mm = (split3, dot6) if exact else (split2, dot3)
        x = split(x)
        x00 = tuple(v[top, top] for v in x)
        x1 = tuple(v[bottom, :] for v in x)
        for copy in copies:
            copy.wait()
        sends = []
        for c, size in enumerate(sizes):
            at = slice(starts[c], starts[c] + size)
            part = split(rows_in[at, :])
            rows_out[at, top] = mm(tuple(v[:, top] for v in part), x00, NT)
            rows_out[at, bottom] = mm(part, x1, NT)
            here = pl.ds(starts[c], size)
            sends.append(pltpu.make_async_copy(rows_out.at[here, :], whitened.at[here, :], sem_out.at[c]))
            sends[-1].start()
        for send in sends:
            send.wait()

    @pl.when(converged)
    def _():
        a = product[...]
        ah = a.astype(BF16)
        product[top, :] = a[top, :] - dot(phi[top, top], ah[top, :], NN)
        product[bottom, :] = a[bottom, :] - dot(phi[bottom, :], ah, NN)
        finish(False)

    @pl.when(jnp.logical_not(converged))
    def _():
        product[...] = gram[...]
        inverse[...] = jnp.where(row == lane, 1.0, 0.0)
        lane_row = lax.broadcasted_iota(jnp.int32, (1, depth), 1)
        row_column = lax.broadcasted_iota(jnp.int32, (depth, 1), 0)

        def eliminate(k, carry):
            pivot_row = product[pl.ds(k, 1), :]
            inverse_row = inverse[pl.ds(k, 1), :]
            pivot = jnp.sum(jnp.where(lane_row == k, pivot_row, 0.0), axis=1, keepdims=True)
            column = jnp.sum(jnp.where(lane == k, product[...], 0.0), axis=1, keepdims=True)
            ratio = jnp.where(row_column > k, column / pivot, 0.0)
            product[...] = product[...] - ratio * pivot_row
            inverse[...] = inverse[...] - ratio * inverse_row
            return carry

        lax.fori_loop(0, depth, eliminate, 0)
        pivots = jnp.sum(jnp.where(row == lane, product[...], 0.0), axis=1, keepdims=True)
        root = 1.0 / jnp.sqrt(pivots)
        product[...] = product[...] * root
        inverse[...] = inverse[...] * root
        finish(True)


def factor_and_apply(halves, pieces, sizes, count, depth, scale):
    rows = sum(sizes)
    size = halves[0].shape[0]

    def kernel(*refs):
        factor_kernel(sizes, count, scale, *refs)

    return pl.pallas_call(
        kernel,
        out_shape=(
            jax.ShapeDtypeStruct((rows, depth), F32),
            jax.ShapeDtypeStruct((depth, depth), F32),
        ),
        in_specs=[VMEM, VMEM] + [HBM] * len(pieces),
        out_specs=(HBM, VMEM),
        scratch_shapes=[
            pltpu.VMEM((2 * size, LANES), F32),
            pltpu.VMEM((depth, depth), F32),
            pltpu.VMEM((depth, depth), BF16),
            pltpu.VMEM((depth, depth), BF16),
            pltpu.VMEM((depth, depth), F32),
            pltpu.VMEM((depth, depth), F32),
            pltpu.VMEM((depth, depth), BF16),
            pltpu.VMEM((rows, depth), F32),
            pltpu.VMEM((rows, depth), F32),
            pltpu.SemaphoreType.DMA((len(pieces),)),
            pltpu.SemaphoreType.DMA((len(sizes),)),
        ],
        compiler_params=pltpu.CompilerParams(vmem_limit_bytes=FACTOR_VMEM),
        cost_estimate=pl.CostEstimate(
            flops=40 * depth**3, bytes_accessed=16 * rows * depth, transcendentals=0
        ),
    )(*halves, *pieces)


def swap(x, axis, distance):
    return lax.ppermute(x, axis, [(i, i ^ distance) for i in range(lax.axis_size(axis))])


def small_call(kernel, out_shape, args):
    several = isinstance(out_shape, list)
    return pl.pallas_call(
        kernel,
        out_shape=out_shape,
        in_specs=[VMEM] * len(args),
        out_specs=[VMEM] * len(out_shape) if several else VMEM,
        compiler_params=pltpu.CompilerParams(vmem_limit_bytes=SMALL_VMEM),
        cost_estimate=pl.CostEstimate(flops=1, bytes_accessed=1 << 20, transcendentals=0),
    )(*args)


def add_and_share(mine, other, count):
    size = mine.shape[0] // count

    def kernel(mine_ref, other_ref, *outs):
        chip = position()[2]
        for k, out in enumerate(outs):
            here = pl.ds(pl.multiple_of((chip ^ k) * size, 8), size)
            out[...] = mine_ref[here, :] + other_ref[here, :]

    shape = jax.ShapeDtypeStruct((size, mine.shape[1]), F32)
    return small_call(kernel, [shape] * count, (mine, other))


def assemble(shares):
    size = shares[0].shape[0]

    def kernel(*refs):
        chip = position()[2]
        for k, ref in enumerate(refs[:-1]):
            refs[-1][pl.ds(pl.multiple_of((chip ^ k) * size, 8), size), :] = ref[...]

    shape = jax.ShapeDtypeStruct((size * len(shares), shares[0].shape[1]), F32)
    return small_call(kernel, shape, shares)


def add_pairs(values):
    while len(values) > 1:
        values = [values[i] + values[i + 1] for i in range(0, len(values), 2)]
    return values[0]


def reduce_blocks(mine, sent):
    chips, count = lax.axis_size("cell") // 2, lax.axis_size("chan")
    shares = add_and_share(mine, swap(sent, "cell", 1), chips)
    x = add_pairs([shares[0]] + [swap(shares[k], "cell", 2 * k) for k in range(1, chips)])
    x = add_pairs([x] + [swap(x, "chan", k) for k in range(1, count)])
    x = assemble([x] + [swap(x, "cell", 2 * k) for k in range(1, chips)])
    return x, swap(x, "cell", 1)


def per_device(embeds):
    count = lax.axis_size("chan")
    z = lax.axis_index("chan")
    rows, width = embeds.shape[0] // count, embeds.shape[1]
    depth = count * width
    if width % LANES == 0:
        sizes = [rows // CHUNKS] * CHUNKS
        offsets = [sum(sizes[:c]) for c in range(CHUNKS)]
        pieces = []
        for c in range(CHUNKS):
            shares = [
                lax.dynamic_slice(embeds, ((z ^ k) * rows + offsets[c], 0), (sizes[c], width))
                for k in range(count)
            ]
            pieces.append([shares[0]] + [swap(shares[k], "chan", k) for k in range(1, count)])
    else:
        whole = lax.all_to_all(embeds, "chan", split_axis=0, concat_axis=1, tiled=True)
        pieces, sizes, count = [[whole]], [rows], 1
    gram = None
    for i, piece in enumerate(pieces):
        gram = partial_gram(piece, gram, i == len(pieces) - 1)
    halves = reduce_blocks(*gram)
    scale = math.sqrt(rows * lax.axis_size("cell") * lax.axis_size("chan"))
    pieces = [v for piece in pieces for v in piece]
    return factor_and_apply(halves, pieces, sizes, count, depth, scale)


def solution(mesh):
    in_specs = (P("cell", "chan"),)
    out_specs = (P(("cell", "chan"), None), P())
    return jax.shard_map(
        per_device, mesh=mesh, in_specs=in_specs, out_specs=out_specs, check_vma=False
    )
```

```python
import math

import jax
import jax.numpy as jnp
from jax import lax
from jax.experimental import pallas as pl
from jax.experimental.pallas import tpu as pltpu
from jax.sharding import PartitionSpec as P


LANES = 128
SHARES = (1, 3, 3, 1)
STEPS = 8
TOL = 3.6e-3
SPREAD = 1.25
GRAM_VMEM = 12 << 20
FACTOR_VMEM = 24 << 20
SMALL_VMEM = 4 << 20
F32 = jnp.float32
BF16 = jnp.bfloat16
VMEM = pl.BlockSpec(memory_space=pltpu.VMEM)
HBM = pl.BlockSpec(memory_space=pltpu.HBM)
NN = ((1,), (0,))
NT = ((1,), (1,))
TN = ((0,), (0,))


def split2(x):
    high = x.astype(BF16)
    return high, (x - high.astype(F32)).astype(BF16)


def split3(x):
    high = x.astype(BF16)
    rest = x - high.astype(F32)
    mid = rest.astype(BF16)
    return high, mid, (rest - mid.astype(F32)).astype(BF16)


def dot(a, b, dims):
    return lax.dot_general(a, b, (dims, ((), ())), preferred_element_type=F32)


def dot3(a, b, dims):
    return dot(a[0], b[1], dims) + dot(a[1], b[0], dims) + dot(a[0], b[0], dims)


def dot6(a, b, dims):
    lhs = jnp.concatenate([a[0], a[2], a[1], a[0], a[1], a[0]], axis=dims[0][0])
    rhs = jnp.concatenate([b[2], b[0], b[1], b[1], b[0], b[0]], axis=dims[1][0])
    return dot(lhs, rhs, dims)


def places(shape=(LANES, LANES)):
    return lax.broadcasted_iota(jnp.int32, shape, 0), lax.broadcasted_iota(jnp.int32, shape, 1)


def layout(n):
    pairs = [(p, q) for p in range(n) for q in range(p + 1, n)]
    offsets = {pq: i * LANES for i, pq in enumerate(pairs)}
    for p in range(0, n, 2):
        offsets[p, p] = (len(pairs) + p // 2) * LANES
    return offsets, (len(pairs) + n // 2) * LANES


def packed_rows(n):
    unit = 8 * lax.axis_size("cell")
    rows = layout(n)[1] + n // 2
    return -(-rows // unit) * unit


def position():
    cell = lax.axis_index("cell")
    return lax.axis_index("chan"), cell & 1, lax.shift_right_logical(cell, 1)


def gram_kernel(count, first, last, *refs):
    z, core, _ = position()
    pieces = refs[:count]
    before = None if first else refs[count]
    refs = refs[count + (0 if first else 1) :]
    if last:
        kept, sent, gram, high, mid, low = refs
    else:
        gram, high, mid, low = refs
    width = pieces[0].shape[1]
    for a in range(count):
        lanes = slice(None)
        if count > 1:
            lanes = pl.ds(pl.multiple_of((z ^ a) * width, width), width)
        high[:, lanes], mid[:, lanes], low[:, lanes] = split3(pieces[a][...])
    n = high.shape[1] // LANES
    offsets, full = layout(n)
    r, c = places()

    def put(at, size, value):
        gram[at : at + size, :] = value if first else before[at : at + size, :] + value

    diagonals = []
    for top in range(0, n, 2):
        rows = slice(top * LANES, (top + 2) * LANES)
        rest = slice(top * LANES, n * LANES)
        lhs = (high[:, rows], mid[:, rows], low[:, rows])
        rhs = (high[:, rest], mid[:, rest], low[:, rest])
        value = dot6(lhs, rhs, TN)

        def block(p, q):
            down, across = (p - top) * LANES, (q - top) * LANES
            return value[down : down + LANES, across : across + LANES]

        for p in (top, top + 1):
            for q in range(p + 1, n):
                put(offsets[p, q], LANES, block(p, q))
        lone = block(top + 1, top + 1)
        put(offsets[top, top], LANES, jnp.where(r <= c, block(top, top), lone))
        diagonals.append(jnp.sum(jnp.where(r == c, lone, 0.0), axis=0, keepdims=True))
    spare = gram.shape[0] - full
    row = lax.broadcasted_iota(jnp.int32, (spare, LANES), 0)
    tail = jnp.zeros((spare, LANES), F32)
    for i, d in enumerate(diagonals):
        tail = jnp.where(row == i, d, tail)
    put(full, spare, tail)
    if last:
        size = kept.shape[0]
        kept[...] = gram[pl.ds(pl.multiple_of(core * size, 8), size), :]
        sent[...] = gram[pl.ds(pl.multiple_of((1 - core) * size, 8), size), :]


def partial_gram(pieces, before, last):
    rows = pieces[0].shape[0]
    depth = sum(p.shape[1] for p in pieces)
    size = packed_rows(depth // LANES)
    args = list(pieces) + ([] if before is None else [before])

    def kernel(*refs):
        gram_kernel(len(pieces), before is None, last, *refs)

    whole = jax.ShapeDtypeStruct((size, LANES), F32)
    part = jax.ShapeDtypeStruct((size // 2, LANES), F32)
    return pl.pallas_call(
        kernel,
        out_shape=(part, part) if last else whole,
        in_specs=[VMEM] * len(args),
        out_specs=(VMEM, VMEM) if last else VMEM,
        scratch_shapes=([pltpu.VMEM((size, LANES), F32)] if last else [])
        + [pltpu.VMEM((rows, depth), BF16)] * 3,
        input_output_aliases={} if before is None or last else {len(args) - 1: 0},
        compiler_params=pltpu.CompilerParams(vmem_limit_bytes=GRAM_VMEM),
        cost_estimate=pl.CostEstimate(
            flops=12 * rows * depth * depth, bytes_accessed=16 * rows * depth, transcendentals=0
        ),
    )(*args)


def factor_kernel(sizes, count, scale, mine, other, *refs):
    z, core, _ = position()
    pieces = refs[: len(sizes) * count]
    refs = refs[len(pieces) :]
    whitened, factor, blocks, gram_high, gram_low, inverse, product, phi = refs[:8]
    rows_in, rows_out, sem_in, sem_out = refs[8:]
    depth = inverse.shape[0]
    n = depth // LANES
    half = depth // 2
    top, bottom = slice(0, half), slice(half, depth)

    starts = [sum(sizes[:i]) for i in range(len(sizes))]
    copies = []
    for i, piece in enumerate(pieces):
        chunk, k = i // count, i % count
        width = piece.shape[1]
        lanes = slice(None)
        if count > 1:
            lanes = pl.ds(pl.multiple_of((z ^ k) * width, width), width)
        target = rows_in.at[pl.ds(starts[chunk], sizes[chunk]), lanes]
        copies.append(pltpu.make_async_copy(piece, target, sem_in.at[i]))
    for copy in copies:
        copy.start()

    size = mine.shape[0]
    blocks[pl.ds(pl.multiple_of(core * size, 8), size), :] = mine[...]
    blocks[pl.ds(pl.multiple_of((1 - core) * size, 8), size), :] = other[...]
    offsets, full = layout(n)
    r, c = places()

    def stored(p, q):
        return blocks[offsets[p, q] : offsets[p, q] + LANES, :]

    def column(line):
        return jnp.sum(jnp.where(r == c, line, 0.0), axis=1, keepdims=True)

    across, down, diagonal = [], [], []
    for p in range(0, n, 2):
        pair = stored(p, p)
        turned = pair.T
        line = blocks[full + p // 2 : full + p // 2 + 1, :]
        diagonal.append(jnp.where(r <= c, pair, turned))
        diagonal.append(jnp.where(r == c, line, jnp.where(r > c, pair, turned)))
        across += [jnp.sum(jnp.where(r == c, pair, 0.0), axis=0, keepdims=True), line]
        down += [column(pair), column(line)]
    across = [lax.rsqrt(v) for v in across]
    down = [lax.rsqrt(v) for v in down]

    def at(p):
        return slice(p * LANES, (p + 1) * LANES)

    def scaled(p, q):
        return (diagonal[p] if p == q else stored(p, q)) * down[p] * across[q]

    zero = jnp.zeros((LANES, LANES), F32)
    for p in range(n):
        for q in range(p, n):
            value = scaled(p, q)
            gram_high[at(p), at(q)], gram_low[at(p), at(q)] = split2(value)
            if p == q:
                inverse[at(p), at(p)] = jnp.where(r == c, 1.0, jnp.where(r > c, -value, 0.0))
            else:
                value = value.T
                gram_high[at(q), at(p)], gram_low[at(q), at(p)] = split2(value)
                inverse[at(q), at(p)] = -value
                inverse[at(p), at(q)] = zero
    wide = jnp.concatenate(across, axis=1)
    unscale = 1.0 / (wide * scale)

    def lower(block):
        i, j = places(block.shape)
        return jnp.where(i > j, block, jnp.where(i == j, 0.5 * block, 0.0))

    def minus_one(block):
        i, j = places(block.shape)
        return jnp.where(i == j, block - 1.0, block)

    def step(three):
        def mm(a, b, dims):
            return dot3(a, b, dims) if three else dot(a[0], b[0], dims)

        x00 = split2(inverse[top, top])
        x1 = split2(inverse[bottom, :])
        a0 = mm(x00, (gram_high[top, :], gram_low[top, :]), NN)
        a1 = mm(x1, (gram_high[...], gram_low[...]), NN)
        product[top, :] = a0
        product[bottom, :] = a1
        a00 = split2(a0[:, top])
        a1s = split2(a1)
        p00 = lower(minus_one(mm(a00, x00, NT)))
        p10 = mm((a1s[0][:, top], a1s[1][:, top]), x00, NT)
        p11 = lower(minus_one(mm(a1s, x1, NT)))
        error = jnp.sum(p00 * p00 + p10 * p10 + p11 * p11)
        h00, h10, h11 = p00.astype(BF16), p10.astype(BF16), p11.astype(BF16)
        p00 -= lower(dot(h00, h00, NT)) + dot(h00, h00, NN)
        p10 -= dot(h10, h00, NT) + dot(h10, h00, NN) + dot(h11, h10, NN)
        p11 -= lower(dot(h10, h10, NT) + dot(h11, h11, NT)) + dot(h11, h11, NN)
        p00, p10, p11 = p00.astype(BF16), p10.astype(BF16), p11.astype(BF16)
        phi[top, top] = p00
        phi[bottom, top] = p10
        phi[bottom, bottom] = p11
        x10, x11 = x1[0][:, top], x1[0][:, bottom]
        y00 = inverse[top, top] - dot(p00, x00[0], NN)
        y10 = inverse[bottom, top] - dot(p10, x00[0], NN) - dot(p11, x10, NN)
        y11 = inverse[bottom, bottom] - dot(p11, x11, NN)
        inverse[top, top] = y00
        inverse[bottom, top] = y10
        inverse[bottom, bottom] = y11
        return error, jnp.sum(y00 * y00 + y10 * y10 + y11 * y11)

    step(False)
    _, error, spread = lax.while_loop(
        lambda s: (s[0] < STEPS) & (s[1] > TOL),
        lambda s: (s[0] + 1,) + step(True),
        (jnp.int32(0), F32(1.0), F32(0.0)),
    )
    converged = (error <= TOL) & (spread <= SPREAD * depth)

    def finish(exact):
        send_factor = pltpu.make_async_copy(product, factor, sem_out.at[len(sizes)])
        send_factor.start()
        split, mm = (split3, dot6) if exact else (split2, dot3)
        x00 = split(inverse[top, top] * (wide[:, top] * scale))
        x1 = split(inverse[bottom, :] * (wide * scale))
        for copy in copies:
            copy.wait()
        sends = []
        for i, size in enumerate(sizes):
            here = slice(starts[i], starts[i] + size)
            part = split(rows_in[here, :])
            rows_out[here, top] = mm(tuple(v[:, top] for v in part), x00, NT)
            rows_out[here, bottom] = mm(part, x1, NT)
            there = pl.ds(starts[i], size)
            sends.append(
                pltpu.make_async_copy(rows_out.at[there, :], whitened.at[there, :], sem_out.at[i])
            )
            sends[-1].start()
        for send in sends:
            send.wait()
        send_factor.wait()

    @pl.when(converged)
    def _():
        def upper(block):
            i, j = places(block.shape)
            return jnp.where(i <= j, block, 0.0)

        a0, a11 = product[top, :], product[bottom, bottom]
        h0, h11 = a0.astype(BF16), a11.astype(BF16)
        r0 = a0 - dot(phi[top, top], h0, NN)
        r11 = a11 - dot(phi[bottom, top], h0[:, bottom], NN) - dot(phi[bottom, bottom], h11, NN)
        product[top, top] = upper(r0[:, top]) * unscale[:, top]
        product[top, bottom] = r0[:, bottom] * unscale[:, bottom]
        product[bottom, top] = jnp.zeros((half, half), F32)
        product[bottom, bottom] = upper(r11) * unscale[:, bottom]
        finish(False)

    @pl.when(jnp.logical_not(converged))
    def _():
        for p in range(n):
            for q in range(p, n):
                value = scaled(p, q)
                product[at(p), at(q)] = value
                if p < q:
                    product[at(q), at(p)] = value.T
        row, lane = places((depth, depth))
        inverse[...] = jnp.where(row == lane, 1.0, 0.0)
        lane_row = lax.broadcasted_iota(jnp.int32, (1, depth), 1)
        row_column = lax.broadcasted_iota(jnp.int32, (depth, 1), 0)

        def eliminate(k, carry):
            pivot_row = product[pl.ds(k, 1), :]
            inverse_row = inverse[pl.ds(k, 1), :]
            pivot = jnp.sum(jnp.where(lane_row == k, pivot_row, 0.0), axis=1, keepdims=True)
            ratio = jnp.sum(jnp.where(lane == k, product[...], 0.0), axis=1, keepdims=True)
            ratio = jnp.where(row_column > k, ratio / pivot, 0.0)
            product[...] = product[...] - ratio * pivot_row
            inverse[...] = inverse[...] - ratio * inverse_row
            return carry

        lax.fori_loop(0, depth, eliminate, 0)
        pivots = jnp.sum(jnp.where(row == lane, product[...], 0.0), axis=1, keepdims=True)
        root = 1.0 / jnp.sqrt(pivots)
        product[...] = jnp.where(row <= lane, product[...] * root, 0.0) * unscale
        inverse[...] = jnp.where(row >= lane, inverse[...] * root, 0.0)
        finish(True)


def factor_and_apply(halves, pieces, sizes, count, depth, scale):
    rows = sum(sizes)
    size = halves[0].shape[0]

    def kernel(*refs):
        factor_kernel(sizes, count, scale, *refs)

    return pl.pallas_call(
        kernel,
        out_shape=(
            jax.ShapeDtypeStruct((rows, depth), F32),
            jax.ShapeDtypeStruct((depth, depth), F32),
        ),
        in_specs=[VMEM, VMEM] + [HBM] * len(pieces),
        out_specs=(HBM, HBM),
        scratch_shapes=[
            pltpu.VMEM((2 * size, LANES), F32),
            pltpu.VMEM((depth, depth), BF16),
            pltpu.VMEM((depth, depth), BF16),
            pltpu.VMEM((depth, depth), F32),
            pltpu.VMEM((depth, depth), F32),
            pltpu.VMEM((depth, depth), BF16),
            pltpu.VMEM((rows, depth), F32),
            pltpu.VMEM((rows, depth), F32),
            pltpu.SemaphoreType.DMA((len(pieces),)),
            pltpu.SemaphoreType.DMA((len(sizes) + 1,)),
        ],
        compiler_params=pltpu.CompilerParams(vmem_limit_bytes=FACTOR_VMEM),
        cost_estimate=pl.CostEstimate(
            flops=40 * depth**3, bytes_accessed=16 * rows * depth, transcendentals=0
        ),
    )(*halves, *pieces)


def swap(x, axis, distance):
    return lax.ppermute(x, axis, [(i, i ^ distance) for i in range(lax.axis_size(axis))])


def small_call(kernel, out_shape, args):
    several = isinstance(out_shape, list)
    return pl.pallas_call(
        kernel,
        out_shape=out_shape,
        in_specs=[VMEM] * len(args),
        out_specs=[VMEM] * len(out_shape) if several else VMEM,
        compiler_params=pltpu.CompilerParams(vmem_limit_bytes=SMALL_VMEM),
        cost_estimate=pl.CostEstimate(flops=1, bytes_accessed=1 << 20, transcendentals=0),
    )(*args)


def add_and_share(mine, other, count):
    size = mine.shape[0] // count

    def kernel(mine_ref, other_ref, *outs):
        chip = position()[2]
        for k, out in enumerate(outs):
            here = pl.ds(pl.multiple_of((chip ^ k) * size, 8), size)
            out[...] = mine_ref[here, :] + other_ref[here, :]

    shape = jax.ShapeDtypeStruct((size, mine.shape[1]), F32)
    return small_call(kernel, [shape] * count, (mine, other))


def assemble(shares):
    size = shares[0].shape[0]

    def kernel(*refs):
        chip = position()[2]
        for k, ref in enumerate(refs[:-1]):
            refs[-1][pl.ds(pl.multiple_of((chip ^ k) * size, 8), size), :] = ref[...]

    shape = jax.ShapeDtypeStruct((size * len(shares), shares[0].shape[1]), F32)
    return small_call(kernel, shape, shares)


def add_pairs(values):
    while len(values) > 1:
        values = [values[i] + values[i + 1] for i in range(0, len(values), 2)]
    return values[0]


def reduce_blocks(mine, sent):
    chips, count = lax.axis_size("cell") // 2, lax.axis_size("chan")
    shares = add_and_share(mine, swap(sent, "cell", 1), chips)
    x = add_pairs([shares[0]] + [swap(shares[k], "cell", 2 * k) for k in range(1, chips)])
    x = add_pairs([x] + [swap(x, "chan", k) for k in range(1, count)])
    x = assemble([x] + [swap(x, "cell", 2 * k) for k in range(1, chips)])
    return x, swap(x, "cell", 1)


def per_device(embeds):
    count = lax.axis_size("chan")
    z = lax.axis_index("chan")
    rows, width = embeds.shape[0] // count, embeds.shape[1]
    depth = count * width
    if width % LANES == 0:
        sizes = [rows * share // sum(SHARES) for share in SHARES]
        offsets = [sum(sizes[:i]) for i in range(len(sizes))]
        pieces = []
        for i, size in enumerate(sizes):
            shares = [
                lax.dynamic_slice(embeds, ((z ^ k) * rows + offsets[i], 0), (size, width))
                for k in range(count)
            ]
            if i < len(sizes) - 1:
                embeds, *shares = lax.optimization_barrier((embeds, *shares))
            pieces.append([shares[0]] + [swap(shares[k], "chan", k) for k in range(1, count)])
    else:
        whole = lax.all_to_all(embeds, "chan", split_axis=0, concat_axis=1, tiled=True)
        pieces, sizes, count = [[whole]], [rows], 1
    gram = None
    for i, piece in enumerate(pieces):
        gram = partial_gram(piece, gram, i == len(pieces) - 1)
    halves = reduce_blocks(*gram)
    scale = math.sqrt(rows * lax.axis_size("cell") * lax.axis_size("chan"))
    pieces = [v for piece in pieces for v in piece]
    return factor_and_apply(halves, pieces, sizes, count, depth, scale)


def solution(mesh):
    in_specs = (P("cell", "chan"),)
    out_specs = (P(("cell", "chan"), None), P())
    return jax.shard_map(
        per_device, mesh=mesh, in_specs=in_specs, out_specs=out_specs, check_vma=False
    )
```

```python
import math

import jax
import jax.numpy as jnp
from jax import lax
from jax.experimental import pallas as pl
from jax.experimental.pallas import tpu as pltpu
from jax.sharding import PartitionSpec as P


LANES = 128
SHARES = (1, 3, 3, 1)
STEPS = 8
TOL = 6e-3
SPREAD = 1.25
GRAM_VMEM = 12 << 20
FACTOR_VMEM = 24 << 20
SMALL_VMEM = 4 << 20
F32 = jnp.float32
BF16 = jnp.bfloat16
VMEM = pl.BlockSpec(memory_space=pltpu.VMEM)
HBM = pl.BlockSpec(memory_space=pltpu.HBM)
NN = ((1,), (0,))
NT = ((1,), (1,))
TN = ((0,), (0,))


def split2(x):
    high = x.astype(BF16)
    return high, (x - high.astype(F32)).astype(BF16)


def split3(x):
    high = x.astype(BF16)
    rest = x - high.astype(F32)
    mid = rest.astype(BF16)
    return high, mid, (rest - mid.astype(F32)).astype(BF16)


def dot(a, b, dims):
    return lax.dot_general(a, b, (dims, ((), ())), preferred_element_type=F32)


def dot3(a, b, dims):
    return dot(a[0], b[1], dims) + dot(a[1], b[0], dims) + dot(a[0], b[0], dims)


def dot6(a, b, dims):
    lhs = jnp.concatenate([a[0], a[2], a[1], a[0], a[1], a[0]], axis=dims[0][0])
    rhs = jnp.concatenate([b[2], b[0], b[1], b[1], b[0], b[0]], axis=dims[1][0])
    return dot(lhs, rhs, dims)


def places(shape=(LANES, LANES)):
    return lax.broadcasted_iota(jnp.int32, shape, 0), lax.broadcasted_iota(jnp.int32, shape, 1)


def layout(n):
    pairs = [(p, q) for p in range(n) for q in range(p + 1, n)]
    offsets = {pq: i * LANES for i, pq in enumerate(pairs)}
    for p in range(0, n, 2):
        offsets[p, p] = (len(pairs) + p // 2) * LANES
    return offsets, (len(pairs) + n // 2) * LANES


def packed_rows(n):
    unit = 8 * lax.axis_size("cell")
    rows = layout(n)[1] + n // 2
    return -(-rows // unit) * unit


def position():
    cell = lax.axis_index("cell")
    return lax.axis_index("chan"), cell & 1, lax.shift_right_logical(cell, 1)


def gram_kernel(count, first, last, *refs):
    z, core, _ = position()
    pieces = refs[:count]
    before = None if first else refs[count]
    refs = refs[count + (0 if first else 1) :]
    if last:
        kept, sent, gram, high, mid, low = refs
    else:
        gram, high, mid, low = refs
    width = pieces[0].shape[1]
    for a in range(count):
        lanes = slice(None)
        if count > 1:
            lanes = pl.ds(pl.multiple_of((z ^ a) * width, width), width)
        high[:, lanes], mid[:, lanes], low[:, lanes] = split3(pieces[a][...])
    n = high.shape[1] // LANES
    offsets, full = layout(n)
    r, c = places()

    def put(at, size, value):
        gram[at : at + size, :] = value if first else before[at : at + size, :] + value

    diagonals = []
    for top in range(0, n, 2):
        rows = slice(top * LANES, (top + 2) * LANES)
        rest = slice(top * LANES, n * LANES)
        lhs = (high[:, rows], mid[:, rows], low[:, rows])
        rhs = (high[:, rest], mid[:, rest], low[:, rest])
        value = dot6(lhs, rhs, TN)

        def block(p, q):
            down, across = (p - top) * LANES, (q - top) * LANES
            return value[down : down + LANES, across : across + LANES]

        for p in (top, top + 1):
            for q in range(p + 1, n):
                put(offsets[p, q], LANES, block(p, q))
        lone = block(top + 1, top + 1)
        put(offsets[top, top], LANES, jnp.where(r <= c, block(top, top), lone))
        diagonals.append(jnp.sum(jnp.where(r == c, lone, 0.0), axis=0, keepdims=True))
    spare = gram.shape[0] - full
    row = lax.broadcasted_iota(jnp.int32, (spare, LANES), 0)
    tail = jnp.zeros((spare, LANES), F32)
    for i, d in enumerate(diagonals):
        tail = jnp.where(row == i, d, tail)
    put(full, spare, tail)
    if last:
        size = kept.shape[0]
        kept[...] = gram[pl.ds(pl.multiple_of(core * size, 8), size), :]
        sent[...] = gram[pl.ds(pl.multiple_of((1 - core) * size, 8), size), :]


def partial_gram(pieces, before, last):
    rows = pieces[0].shape[0]
    depth = sum(p.shape[1] for p in pieces)
    size = packed_rows(depth // LANES)
    args = list(pieces) + ([] if before is None else [before])

    def kernel(*refs):
        gram_kernel(len(pieces), before is None, last, *refs)

    whole = jax.ShapeDtypeStruct((size, LANES), F32)
    part = jax.ShapeDtypeStruct((size // 2, LANES), F32)
    return pl.pallas_call(
        kernel,
        out_shape=(part, part) if last else whole,
        in_specs=[VMEM] * len(args),
        out_specs=(VMEM, VMEM) if last else VMEM,
        scratch_shapes=([pltpu.VMEM((size, LANES), F32)] if last else [])
        + [pltpu.VMEM((rows, depth), BF16)] * 3,
        input_output_aliases={} if before is None or last else {len(args) - 1: 0},
        compiler_params=pltpu.CompilerParams(vmem_limit_bytes=GRAM_VMEM),
        cost_estimate=pl.CostEstimate(
            flops=12 * rows * depth * depth, bytes_accessed=16 * rows * depth, transcendentals=0
        ),
    )(*args)


def factor_kernel(sizes, count, scale, mine, other, *refs):
    z, core, _ = position()
    pieces = refs[: len(sizes) * count]
    refs = refs[len(pieces) :]
    whitened, factor, blocks, gram_high, gram_low, inverse, product = refs[:7]
    rows_in, rows_out, sem_in, sem_out = refs[7:]
    depth = inverse.shape[0]
    n = depth // LANES
    half = depth // 2
    top, bottom = slice(0, half), slice(half, depth)

    starts = [sum(sizes[:i]) for i in range(len(sizes))]
    copies = []
    for i, piece in enumerate(pieces):
        chunk, k = i // count, i % count
        width = piece.shape[1]
        lanes = slice(None)
        if count > 1:
            lanes = pl.ds(pl.multiple_of((z ^ k) * width, width), width)
        target = rows_in.at[pl.ds(starts[chunk], sizes[chunk]), lanes]
        copies.append(pltpu.make_async_copy(piece, target, sem_in.at[i]))
    for copy in copies:
        copy.start()

    size = mine.shape[0]
    blocks[pl.ds(pl.multiple_of(core * size, 8), size), :] = mine[...]
    blocks[pl.ds(pl.multiple_of((1 - core) * size, 8), size), :] = other[...]
    offsets, full = layout(n)
    r, c = places()

    def stored(p, q):
        return blocks[offsets[p, q] : offsets[p, q] + LANES, :]

    def column(line):
        return jnp.sum(jnp.where(r == c, line, 0.0), axis=1, keepdims=True)

    across, down, diagonal = [], [], []
    for p in range(0, n, 2):
        pair = stored(p, p)
        turned = pair.T
        line = blocks[full + p // 2 : full + p // 2 + 1, :]
        diagonal.append(jnp.where(r <= c, pair, turned))
        diagonal.append(jnp.where(r == c, line, jnp.where(r > c, pair, turned)))
        across += [jnp.sum(jnp.where(r == c, pair, 0.0), axis=0, keepdims=True), line]
        down += [column(pair), column(line)]
    across = [lax.rsqrt(v) for v in across]
    down = [lax.rsqrt(v) for v in down]

    def at(p):
        return slice(p * LANES, (p + 1) * LANES)

    def scaled(p, q):
        return (diagonal[p] if p == q else stored(p, q)) * down[p] * across[q]

    zero = jnp.zeros((LANES, LANES), F32)
    for p in range(n):
        for q in range(p, n):
            value = scaled(p, q)
            gram_high[at(p), at(q)], gram_low[at(p), at(q)] = split2(value)
            if p == q:
                inverse[at(p), at(p)] = jnp.where(r == c, 1.0, jnp.where(r > c, -value, 0.0))
            else:
                value = value.T
                gram_high[at(q), at(p)], gram_low[at(q), at(p)] = split2(value)
                inverse[at(q), at(p)] = -value
                inverse[at(p), at(q)] = zero
    wide = jnp.concatenate(across, axis=1)
    unscale = 1.0 / (wide * scale)

    def lower(block):
        i, j = places(block.shape)
        return jnp.where(i > j, block, jnp.where(i == j, 0.5 * block, 0.0))

    def minus_one(block):
        i, j = places(block.shape)
        return jnp.where(i == j, block - 1.0, block)

    def step(three):
        def mm(a, b, dims):
            return dot3(a, b, dims) if three else dot(a[0], b[0], dims)

        x00 = split2(inverse[top, top])
        x1 = split2(inverse[bottom, :])
        a0 = mm(x00, (gram_high[top, :], gram_low[top, :]), NN)
        a1 = mm(x1, (gram_high[...], gram_low[...]), NN)
        a00 = split2(a0[:, top])
        a1s = split2(a1)
        p00 = lower(minus_one(mm(a00, x00, NT)))
        p10 = mm((a1s[0][:, top], a1s[1][:, top]), x00, NT)
        p11 = lower(minus_one(mm(a1s, x1, NT)))
        error = jnp.sum(p00 * p00 + p10 * p10 + p11 * p11)
        if three:
            h00, h10, h11 = p00.astype(BF16), p10.astype(BF16), p11.astype(BF16)
            p00 -= lower(dot(h00, h00, NT)) + dot(h00, h00, NN)
            p10 -= dot(h10, h00, NT) + dot(h10, h00, NN) + dot(h11, h10, NN)
            p11 -= lower(dot(h10, h10, NT) + dot(h11, h11, NT)) + dot(h11, h11, NN)
        p00, p10, p11 = p00.astype(BF16), p10.astype(BF16), p11.astype(BF16)
        if three:
            a11 = a1[:, bottom]
            product[top, :] = a0 - dot(p00, a0.astype(BF16), NN)
            product[bottom, bottom] = (
                a11 - dot(p10, a0[:, bottom].astype(BF16), NN) - dot(p11, a1s[0][:, bottom], NN)
            )
        x10, x11 = x1[0][:, top], x1[0][:, bottom]
        y00 = inverse[top, top] - dot(p00, x00[0], NN)
        y10 = inverse[bottom, top] - dot(p10, x00[0], NN) - dot(p11, x10, NN)
        y11 = inverse[bottom, bottom] - dot(p11, x11, NN)
        inverse[top, top] = y00
        inverse[bottom, top] = y10
        inverse[bottom, bottom] = y11
        return error, jnp.sum(y00 * y00 + y10 * y10 + y11 * y11)

    step(False)
    _, error, spread = lax.while_loop(
        lambda s: (s[0] < STEPS) & (s[1] > TOL),
        lambda s: (s[0] + 1,) + step(True),
        (jnp.int32(0),) + step(True),
    )
    converged = (error <= TOL) & (spread <= SPREAD * depth)

    def finish(exact):
        send_factor = pltpu.make_async_copy(product, factor, sem_out.at[len(sizes)])
        send_factor.start()
        split, mm = (split3, dot6) if exact else (split2, dot3)
        x00 = split(inverse[top, top] * (wide[:, top] * scale))
        x1 = split(inverse[bottom, :] * (wide * scale))
        for copy in copies:
            copy.wait()
        sends = []
        for i, size in enumerate(sizes):
            here = slice(starts[i], starts[i] + size)
            part = split(rows_in[here, :])
            rows_out[here, top] = mm(tuple(v[:, top] for v in part), x00, NT)
            rows_out[here, bottom] = mm(part, x1, NT)
            there = pl.ds(starts[i], size)
            sends.append(
                pltpu.make_async_copy(rows_out.at[there, :], whitened.at[there, :], sem_out.at[i])
            )
            sends[-1].start()
        for send in sends:
            send.wait()
        send_factor.wait()

    @pl.when(converged)
    def _():
        def upper(block):
            i, j = places(block.shape)
            return jnp.where(i <= j, block, 0.0)

        product[top, top] = upper(product[top, top]) * unscale[:, top]
        product[top, bottom] = product[top, bottom] * unscale[:, bottom]
        product[bottom, top] = jnp.zeros((half, half), F32)
        product[bottom, bottom] = upper(product[bottom, bottom]) * unscale[:, bottom]
        finish(False)

    @pl.when(jnp.logical_not(converged))
    def _():
        for p in range(n):
            for q in range(p, n):
                value = scaled(p, q)
                product[at(p), at(q)] = value
                if p < q:
                    product[at(q), at(p)] = value.T
        row, lane = places((depth, depth))
        inverse[...] = jnp.where(row == lane, 1.0, 0.0)
        lane_row = lax.broadcasted_iota(jnp.int32, (1, depth), 1)
        row_column = lax.broadcasted_iota(jnp.int32, (depth, 1), 0)

        def eliminate(k, carry):
            pivot_row = product[pl.ds(k, 1), :]
            inverse_row = inverse[pl.ds(k, 1), :]
            pivot = jnp.sum(jnp.where(lane_row == k, pivot_row, 0.0), axis=1, keepdims=True)
            ratio = jnp.sum(jnp.where(lane == k, product[...], 0.0), axis=1, keepdims=True)
            ratio = jnp.where(row_column > k, ratio / pivot, 0.0)
            product[...] = product[...] - ratio * pivot_row
            inverse[...] = inverse[...] - ratio * inverse_row
            return carry

        lax.fori_loop(0, depth, eliminate, 0)
        pivots = jnp.sum(jnp.where(row == lane, product[...], 0.0), axis=1, keepdims=True)
        root = 1.0 / jnp.sqrt(pivots)
        product[...] = jnp.where(row <= lane, product[...] * root, 0.0) * unscale
        inverse[...] = jnp.where(row >= lane, inverse[...] * root, 0.0)
        finish(True)


def factor_and_apply(halves, pieces, sizes, count, depth, scale):
    rows = sum(sizes)
    size = halves[0].shape[0]

    def kernel(*refs):
        factor_kernel(sizes, count, scale, *refs)

    return pl.pallas_call(
        kernel,
        out_shape=(
            jax.ShapeDtypeStruct((rows, depth), F32),
            jax.ShapeDtypeStruct((depth, depth), F32),
        ),
        in_specs=[VMEM, VMEM] + [HBM] * len(pieces),
        out_specs=(HBM, HBM),
        scratch_shapes=[
            pltpu.VMEM((2 * size, LANES), F32),
            pltpu.VMEM((depth, depth), BF16),
            pltpu.VMEM((depth, depth), BF16),
            pltpu.VMEM((depth, depth), F32),
            pltpu.VMEM((depth, depth), F32),
            pltpu.VMEM((rows, depth), F32),
            pltpu.VMEM((rows, depth), F32),
            pltpu.SemaphoreType.DMA((len(pieces),)),
            pltpu.SemaphoreType.DMA((len(sizes) + 1,)),
        ],
        compiler_params=pltpu.CompilerParams(vmem_limit_bytes=FACTOR_VMEM),
        cost_estimate=pl.CostEstimate(
            flops=40 * depth**3, bytes_accessed=16 * rows * depth, transcendentals=0
        ),
    )(*halves, *pieces)


def swap(x, axis, distance):
    return lax.ppermute(x, axis, [(i, i ^ distance) for i in range(lax.axis_size(axis))])


def small_call(kernel, out_shape, args):
    several = isinstance(out_shape, list)
    return pl.pallas_call(
        kernel,
        out_shape=out_shape,
        in_specs=[VMEM] * len(args),
        out_specs=[VMEM] * len(out_shape) if several else VMEM,
        compiler_params=pltpu.CompilerParams(vmem_limit_bytes=SMALL_VMEM),
        cost_estimate=pl.CostEstimate(flops=1, bytes_accessed=1 << 20, transcendentals=0),
    )(*args)


def add_and_share(mine, other, count):
    size = mine.shape[0] // count

    def kernel(mine_ref, other_ref, *outs):
        chip = position()[2]
        for k, out in enumerate(outs):
            here = pl.ds(pl.multiple_of((chip ^ k) * size, 8), size)
            out[...] = mine_ref[here, :] + other_ref[here, :]

    shape = jax.ShapeDtypeStruct((size, mine.shape[1]), F32)
    return small_call(kernel, [shape] * count, (mine, other))


def assemble(shares):
    size = shares[0].shape[0]

    def kernel(*refs):
        chip = position()[2]
        for k, ref in enumerate(refs[:-1]):
            refs[-1][pl.ds(pl.multiple_of((chip ^ k) * size, 8), size), :] = ref[...]

    shape = jax.ShapeDtypeStruct((size * len(shares), shares[0].shape[1]), F32)
    return small_call(kernel, shape, shares)


def add_pairs(values):
    while len(values) > 1:
        values = [values[i] + values[i + 1] for i in range(0, len(values), 2)]
    return values[0]


def reduce_blocks(mine, sent):
    chips, count = lax.axis_size("cell") // 2, lax.axis_size("chan")
    shares = add_and_share(mine, swap(sent, "cell", 1), chips)
    x = add_pairs([shares[0]] + [swap(shares[k], "cell", 2 * k) for k in range(1, chips)])
    x = add_pairs([x] + [swap(x, "chan", k) for k in range(1, count)])
    x = assemble([x] + [swap(x, "cell", 2 * k) for k in range(1, chips)])
    return x, swap(x, "cell", 1)


def per_device(embeds):
    count = lax.axis_size("chan")
    z = lax.axis_index("chan")
    rows, width = embeds.shape[0] // count, embeds.shape[1]
    depth = count * width
    if width % LANES == 0:
        sizes = [rows * share // sum(SHARES) for share in SHARES]
        offsets = [sum(sizes[:i]) for i in range(len(sizes))]
        pieces = []
        for i, size in enumerate(sizes):
            shares = [
                lax.dynamic_slice(embeds, ((z ^ k) * rows + offsets[i], 0), (size, width))
                for k in range(count)
            ]
            if i < len(sizes) - 1:
                embeds, *shares = lax.optimization_barrier((embeds, *shares))
            pieces.append([shares[0]] + [swap(shares[k], "chan", k) for k in range(1, count)])
    else:
        whole = lax.all_to_all(embeds, "chan", split_axis=0, concat_axis=1, tiled=True)
        pieces, sizes, count = [[whole]], [rows], 1
    gram = None
    for i, piece in enumerate(pieces):
        gram = partial_gram(piece, gram, i == len(pieces) - 1)
    halves = reduce_blocks(*gram)
    scale = math.sqrt(rows * lax.axis_size("cell") * lax.axis_size("chan"))
    pieces = [v for piece in pieces for v in piece]
    return factor_and_apply(halves, pieces, sizes, count, depth, scale)


def solution(mesh):
    in_specs = (P("cell", "chan"),)
    out_specs = (P(("cell", "chan"), None), P())
    return jax.shard_map(
        per_device, mesh=mesh, in_specs=in_specs, out_specs=out_specs, check_vma=False
    )
```
